1024 devices in a mesh: grp: 16 (over y, x), mdl: 64 (over z, core).
Axes of the slice: x: 4, y: 4, z: 32, core: 2. Of those that a mesh axis runs over, the one named last changes fastest.
Arguments:
- enc_out: bfloat16 [5120, 8192], P('grp'), may hold values from -6 to 6
- w_key: bfloat16 [8192, 8192], P(None, 'mdl'), may hold values from -0.0625 to 0.0625
- w_value: bfloat16 [8192, 8192], P(None, 'mdl'), may hold values from -0.0625 to 0.0625
- queries: bfloat16 [24576, 8192], P('grp', 'mdl'), may hold values from -600 to 600
- src_len: int32 [16, 19], replicated, may hold values from 1 to 48, as said below
- tgt_len: int32 [304], replicated, may hold values from 1 to 48, as said below
- destination: int32 [304, 1], replicated, may hold values from 0 to 15
Outputs:
- context: bfloat16 [24576, 8192], P('grp', 'mdl')
- variance: float32 [], replicated
The draws below stay inside these ranges and needn't reach their ends.
Inputs may be any that keep to these rules, and one draw needn't show every extreme that they name: `src_len`: the sentences of one encoder shard fill its 320 rows, one of them has 48 rows, and the sentences of one shard with one destination have at most 96 source rows, reached by some group for every shard. `tgt_len`: the sentences of one shard with one destination have as many target rows in all as source rows.
All inputs are finite; a program needn't handle non-finite values.
Results may differ from the reference program's by a relative error of at most 0.024.
Values may be sent and summed in bfloat16 or wider, within the bound.
A program may use at most 32 MiB of HBM per device.

```python
import jax
import jax.numpy as jnp
from jax import lax

D = 8192
HEADS = 64
HEAD_DIM = 128
MEAN_LEN = 16
UNITS = 10
SRC_DEV = 320
MAX_LEN = 48
CAP = 96
SENTS = 19
ROWS_GROUP = 1536
SRC_ROWS = 5120
TGT_ROWS = 24576
N_GRP = 16


def split_lengths(key_a, key_x, key_c, rest):
    first = jax.random.randint(key_a, (1,), 1, 2 * MEAN_LEN, dtype=jnp.int32)
    second = jax.random.randint(key_x, (1,), 1, MEAN_LEN, dtype=jnp.int32)
    others = jax.random.randint(key_c, (rest,), 1, 2 * MEAN_LEN, dtype=jnp.int32)
    longest = jnp.zeros((1,), jnp.int32) + MAX_LEN
    heavy = jnp.concatenate([longest, first, 2 * MEAN_LEN - first, second, MEAN_LEN - second])
    return jnp.concatenate([heavy, others, 2 * MEAN_LEN - others])


def joint_draw(key):
    base = jax.random.fold_in(key, 77)
    rest = UNITS - 3

    def one_shard(shard):
        shard_key = jax.random.fold_in(base, shard)
        keys = jax.random.split(shard_key, 8)
        order_groups = jax.random.permutation(keys[0], N_GRP).astype(jnp.int32)
        picks = 1 + jnp.arange(rest, dtype=jnp.int32) % (N_GRP - 1)
        rest_groups = order_groups[picks]
        heavy_groups = jnp.zeros((5,), jnp.int32) + order_groups[0]
        groups = jnp.concatenate([heavy_groups, rest_groups, rest_groups])
        source = split_lengths(keys[1], keys[2], keys[3], rest)
        target = split_lengths(keys[4], keys[5], keys[6], rest)
        order = jax.random.permutation(keys[7], SENTS).astype(jnp.int32)
        return (source[order], target[order], groups[order])
    return jax.vmap(one_shard)(jnp.arange(N_GRP, dtype=jnp.int32))


def draw_src_len(key, part):
    source, target, groups = joint_draw(key)
    return source.astype(jnp.int32)


def draw_tgt_len(key, part):
    source, target, groups = joint_draw(key)
    return target.reshape(-1).astype(jnp.int32)


def draw_destination(key, part):
    source, target, groups = joint_draw(key)
    return groups.reshape(-1, 1).astype(jnp.int32)


def draw_queries(key, part):
    values = jax.random.normal(jax.random.fold_in(key, 11), (TGT_ROWS, D), jnp.float32)
    values = jnp.clip(values, -6.0, 6.0)
    return values.astype(jnp.bfloat16)


def block_scale(key, shape, cuts, low, high):
    def one(position, blocks):
        draws = jax.random.uniform(jax.random.fold_in(jax.random.fold_in(key, 6), position), (blocks,), jnp.float32, low / len(cuts), high / len(cuts))
        return jnp.repeat(jnp.exp(draws), shape[position] // blocks).reshape((-1,) + (1,) * (len(shape) - position - 1))

    gain = one(*cuts[0])
    for cut in cuts[1:]:
        gain = gain * one(*cut)
    return gain


def normal_values(key, extent, width, reach, cuts=(), kind=jnp.bfloat16):
    gain = block_scale(key, extent, cuts, -0.22, 0.18) if cuts else 1.0
    array = jax.random.normal(key, extent, jnp.float32) * width * gain
    return jnp.minimum(jnp.maximum(array, -reach), reach).astype(kind)


def setup_inputs(seed: int = 0) -> dict:
    streams_of = jax.random.split(jax.random.key(seed), 8)
    enc_out = normal_values(streams_of[0], (SRC_ROWS, D), 1.0, 6.0, ((0, 16),))
    w_key = normal_values(streams_of[1], (D, D), D ** -0.5, 0.0625, ((1, 64),))
    w_value = normal_values(streams_of[2], (D, D), D ** -0.5, 0.0625, ((1, 64),))
    queries = draw_queries(jax.random.fold_in(streams_of[7], 71), 0)
    src_len = draw_src_len(jax.random.fold_in(streams_of[7], 71), 0)
    tgt_len = draw_tgt_len(jax.random.fold_in(streams_of[7], 71), 0)
    destination = draw_destination(jax.random.fold_in(streams_of[7], 71), 0)
    return {"enc_out": enc_out, "w_key": w_key, "w_value": w_value, "queries": queries, "src_len": src_len, "tgt_len": tgt_len, "destination": destination}


def layout(lengths, groups_of, wanted):
    going = (groups_of == wanted[:, None]).astype(jnp.int32)
    sent = lengths * going
    pair_start = jnp.cumsum(sent, axis=1) - sent
    rows = jnp.arange(CAP, dtype=jnp.int32)[None, :, None]
    above = (rows >= pair_start[:, None, :]).astype(jnp.int32)
    below = (rows < (pair_start + lengths)[:, None, :]).astype(jnp.int32)
    return going[:, None, :] * above * below, pair_start


def describe(member):
    numbers = jnp.arange(member.shape[2], dtype=jnp.int32)
    return jnp.sum(member, axis=2), jnp.sum(member * numbers[None, None, :], axis=2)


def attend(query_block, key_block, value_block, q_live, q_seg, k_live, k_seg):
    scores = jnp.einsum('eqhd,ekhd->ehqk', query_block.astype(jnp.float32), key_block.astype(jnp.float32)) * (HEAD_DIM ** -0.5)
    allowed = (q_live[:, :, None] > 0) & (k_live[:, None, :] > 0) & (q_seg[:, :, None] == k_seg[:, None, :])
    allowed = allowed[:, None]
    scores = jnp.where(allowed, scores, -1e30)
    top = jnp.max(scores, axis=-1, keepdims=True)
    powers = jnp.where(allowed, jnp.exp(scores - top), 0.0)
    dead = (1 - q_live).astype(jnp.float32)[:, None, :, None]
    total = jnp.sum(powers, axis=-1, keepdims=True) + dead
    weights = (powers / total).astype(jnp.bfloat16)
    attended = jnp.einsum('ehqk,ekhd->eqhd', weights.astype(jnp.float32), value_block.astype(jnp.float32))
    return attended * q_live.astype(jnp.float32)[:, :, None, None]


def reference(enc_out, w_key, w_value, queries, src_len, tgt_len, destination):
    key_states = jnp.dot(enc_out, w_key, preferred_element_type=jnp.float32).astype(jnp.bfloat16)
    value_states = jnp.dot(enc_out, w_value, preferred_element_type=jnp.float32).astype(jnp.bfloat16)
    shards = src_len.shape[0]
    groups_of = destination.reshape(shards, SENTS)
    starts = jnp.cumsum(src_len, axis=1) - src_len
    targets = tgt_len.reshape(shards, SENTS)
    shard_ids = jnp.arange(shards, dtype=jnp.int32)
    rows = jnp.arange(CAP, dtype=jnp.int32)

    def one_group(group):
        wanted = jnp.zeros((shards,), jnp.int32) + group
        member_src, pair_src = layout(src_len, groups_of, wanted)
        k_live, k_seg = describe(member_src)
        offset = jnp.sum(member_src * (starts - pair_src)[:, None, :], axis=2) + rows[None, :]
        row_index = jnp.clip(shard_ids[:, None] * SRC_DEV + offset, 0, shards * SRC_DEV - 1).astype(jnp.int32)
        member_tgt, pair_tgt = layout(targets, groups_of, wanted)
        q_live, q_seg = describe(member_tgt)
        key_block = jnp.take(key_states, row_index.reshape(-1), axis=0).reshape(shards, CAP, HEADS, HEAD_DIM)
        value_block = jnp.take(value_states, row_index.reshape(-1), axis=0).reshape(shards, CAP, HEADS, HEAD_DIM)
        query_block = lax.dynamic_slice_in_dim(queries, (group * ROWS_GROUP).astype(jnp.int32), ROWS_GROUP, 0)
        query_block = query_block.reshape(shards, CAP, HEADS, HEAD_DIM)
        attended = attend(query_block, key_block, value_block, q_live, q_seg, k_live, k_seg)
        return attended.reshape(ROWS_GROUP, D).astype(jnp.bfloat16), jnp.sum(attended * attended)

    context, squares = lax.map(one_group, shard_ids)
    variance = jnp.sum(squares) / (jnp.float32(D) * jnp.sum(tgt_len).astype(jnp.float32))
    return context.reshape(shards * ROWS_GROUP, D), variance
```

```python
import functools
import math

import jax
import jax.numpy as jnp
from jax import lax
from jax.experimental import pallas as pl
from jax.experimental.pallas import tpu as pltpu
from jax.sharding import PartitionSpec as P

HEAD_DIM = 128
CAP = 96
SENTS = 19
CHUNKS = 8
BATCH = 4
MESH = pl.DeviceIdType.MESH
SCALE = math.log2(math.e) * HEAD_DIM**-0.5


def kernel(
    ng, nm, ni,
    enc, wk, wv, q, src, tgt, dst,
    ctx, var,
    enc_v, w_v, q_v, c_v, seg_v, r1, r2, r3, src_s, tgt_s, dst_s,
    load_sem, small_sem, qs_sem, qr_sem, cs_sem, cr_sem, own_sem,
    s1_sem, t1_sem, s2_sem, t2_sem, s3_sem, t3_sem,
):
    me = lax.axis_index("grp")
    mm = lax.axis_index("mdl")
    rows, depth = enc.shape
    kc = depth // CHUNKS
    no = nm // ni

    small = [
        pltpu.make_async_copy(a, b, small_sem.at[i])
        for i, (a, b) in enumerate(((src, src_s), (tgt, tgt_s), (dst, dst_s)))
    ]
    for copy in small:
        copy.start()

    def loads(c):
        part = pl.ds(c * kc, kc)
        return (
            pltpu.make_async_copy(enc.at[:, part], enc_v.at[c], load_sem.at[0, c]),
            pltpu.make_async_copy(wk.at[part], w_v.at[part, pl.ds(0, HEAD_DIM)], load_sem.at[1, c]),
            pltpu.make_async_copy(
                wv.at[part], w_v.at[part, pl.ds(HEAD_DIM, HEAD_DIM)], load_sem.at[2, c]
            ),
        )

    own_rows = pl.ds(pl.multiple_of(me * CAP, 32), CAP)
    own_q = pltpu.make_async_copy(q.at[own_rows], q_v.at[0], own_sem.at[0])
    own_q.start()
    for c in range(CHUNKS):
        for copy in loads(c):
            copy.start()

    def grp_peer(d):
        return {"grp": lax.rem(me + d, ng)}

    inner, outer = lax.rem(mm, ni), mm // ni

    def in_peer(d):
        return {"mdl": outer * ni + lax.rem(inner + d, ni)}

    def out_peer(d):
        return {"mdl": lax.rem(outer + d, no) * ni + inner}

    barrier = pltpu.get_barrier_semaphore()
    for d in range(1, ng):
        pl.semaphore_signal(barrier, inc=1, device_id=grp_peer(d), device_id_type=MESH)
    for d in range(1, ni):
        pl.semaphore_signal(barrier, inc=1, device_id=in_peer(d), device_id_type=MESH)
    for d in range(1, no):
        pl.semaphore_signal(barrier, inc=1, device_id=out_peer(d), device_id_type=MESH)
    pl.semaphore_wait(barrier, (ng - 1) + (ni - 1) + (no - 1))

    def query_copy(d):
        peer = lax.rem(me + d, ng)
        return pltpu.make_async_remote_copy(
            src_ref=q.at[pl.ds(pl.multiple_of(peer * CAP, 32), CAP)],
            dst_ref=q_v.at[d],
            send_sem=qs_sem.at[d],
            recv_sem=qr_sem.at[d],
            device_id={"grp": peer},
            device_id_type=MESH,
        )

    for d in range(1, ng):
        query_copy(d).start()

    for copy in small:
        copy.wait()
    slot = lax.broadcasted_iota(jnp.int32, seg_v.shape[::-1], 0)
    lane = lax.broadcasted_iota(jnp.int32, seg_v.shape[::-1], 1)
    group_of = lax.rem(me + ng - slot % ng, ng)
    key_row = lax.broadcasted_iota(jnp.int32, (1, rows), 1)
    seg_q = jnp.full(slot.shape, -1.0, jnp.float32)
    seg_k = jnp.zeros((1, rows), jnp.float32)
    filled = jnp.zeros(slot.shape, jnp.int32)
    start = jnp.int32(0)
    for i in range(SENTS):
        count = tgt_s[me * SENTS + i]
        going = group_of == dst_s[0, me * SENTS + i]
        after = jnp.where(going, filled + count, filled)
        seg_q = jnp.where((lane >= filled) & (lane < after), float(i), seg_q)
        filled = after
        seg_k = jnp.where(key_row >= start, float(i), seg_k)
        start = start + src_s[me, i]
    side = seg_v.shape[0]
    eye = (
        lax.broadcasted_iota(jnp.int32, (side, side), 0)
        == lax.broadcasted_iota(jnp.int32, (side, side), 1)
    ).astype(jnp.float32).astype(jnp.bfloat16)
    seg_v[...] = lax.dot_general(
        eye, seg_q.astype(jnp.bfloat16), (((1,), (1,)), ((), ())),
        preferred_element_type=jnp.float32,
    )
    live_rows = lax.fori_loop(
        0, tgt.shape[0], lambda i, t: t + tgt_s[i], jnp.int32(0), unroll=8
    )

    total = jnp.zeros((rows, 2 * HEAD_DIM), jnp.float32)
    for c in range(CHUNKS):
        for copy in loads(c):
            copy.wait()
        total = total + jnp.dot(
            enc_v[c], w_v[pl.ds(c * kc, kc), :], preferred_element_type=jnp.float32
        )
    keys = total[:, :HEAD_DIM].astype(jnp.bfloat16)
    values = jnp.concatenate(
        [total[:, HEAD_DIM:].astype(jnp.bfloat16), jnp.ones((rows, HEAD_DIM), jnp.bfloat16)], axis=1
    )

    def context_copy(d):
        return pltpu.make_async_remote_copy(
            src_ref=c_v.at[d],
            dst_ref=ctx.at[own_rows],
            send_sem=cs_sem.at[d],
            recv_sem=cr_sem.at[d],
            device_id={"grp": lax.rem(me + ng - d, ng)},
            device_id_type=MESH,
        )

    squares = jnp.zeros((8, HEAD_DIM), jnp.float32)
    own_c = pltpu.make_async_copy(c_v.at[0], ctx.at[own_rows], own_sem.at[1])
    for first in range(0, ng, BATCH):
        slots = range(first, first + BATCH)
        for d in slots:
            if d == 0:
                own_q.wait()
            else:
                query_copy(d).wait_recv()
        block = q_v[first : first + BATCH].reshape(BATCH * CAP, HEAD_DIM)
        seg = jnp.concatenate([seg_v[0:CAP, d : d + 1] for d in slots], axis=0)
        scores = lax.dot_general(
            block, keys, (((1,), (1,)), ((), ())), preferred_element_type=jnp.float32
        )
        scores = jnp.where(seg == seg_k, scores, -1e30)
        top = jnp.max(scores, axis=1, keepdims=True)
        powers = jnp.exp2((scores - top) * SCALE).astype(jnp.bfloat16)
        both = jnp.dot(powers, values, preferred_element_type=jnp.float32)
        attended = both[:, :HEAD_DIM] / both[:, HEAD_DIM:]
        attended = jnp.where(seg >= 0.0, attended, 0.0)
        c_v[first : first + BATCH] = attended.astype(jnp.bfloat16).reshape(BATCH, CAP, HEAD_DIM)
        squares = squares + jnp.sum(
            (attended * attended).reshape(BATCH * CAP // 8, 8, HEAD_DIM), axis=0
        )
        for d in slots:
            if d == 0:
                own_c.start()
            else:
                context_copy(d).start()

    def add_up(value, slots_ref, send_sem, recv_sem, count, peer):
        slots_ref[0] = value

        def copy(d):
            return pltpu.make_async_remote_copy(
                src_ref=slots_ref.at[0],
                dst_ref=slots_ref.at[d],
                send_sem=send_sem.at[d],
                recv_sem=recv_sem.at[d],
                device_id=peer(d),
                device_id_type=MESH,
            )

        for d in range(1, count):
            copy(d).start()
        for d in range(1, count):
            copy(d).wait_recv()
        out = jnp.sum(slots_ref[...], axis=0)
        return out, [copy(d) for d in range(1, count)]

    squares, sent1 = add_up(squares, r1, s1_sem, t1_sem, ni, in_peer)
    squares, sent2 = add_up(squares, r2, s2_sem, t2_sem, no, out_peer)
    squares, sent3 = add_up(squares, r3, s3_sem, t3_sem, ng, grp_peer)
    width = jnp.float32(HEAD_DIM * nm)
    var[...] = jnp.full(
        var.shape, jnp.sum(squares) / (width * live_rows.astype(jnp.float32)), jnp.float32
    )

    own_c.wait()
    for d in range(1, ng):
        query_copy(d).wait_send()
        context_copy(d).wait()
    for copy in sent1 + sent2 + sent3:
        copy.wait_send()


def per_device(ng, nm, enc_out, w_key, w_value, queries, src_len, tgt_len, destination):
    ni = math.gcd(nm, 8) if nm > 8 else max(nm // 2, 1)
    no = nm // ni
    rows, depth = enc_out.shape
    hbm = pl.BlockSpec(memory_space=pltpu.HBM)
    dma = pltpu.SemaphoreType.DMA
    context, variance = pl.pallas_call(
        functools.partial(kernel, ng, nm, ni),
        name="attend",
        out_shape=(
            jax.ShapeDtypeStruct(queries.shape, jnp.bfloat16),
            jax.ShapeDtypeStruct((1, 1), jnp.float32),
        ),
        in_specs=[hbm] * 7,
        out_specs=(pl.BlockSpec(memory_space=pl.ANY), pl.BlockSpec(memory_space=pltpu.VMEM)),
        scratch_shapes=[
            pltpu.VMEM((CHUNKS, rows, depth // CHUNKS), jnp.bfloat16),
            pltpu.VMEM((depth, 2 * HEAD_DIM), jnp.bfloat16),
            pltpu.VMEM((ng, CAP, HEAD_DIM), jnp.bfloat16),
            pltpu.VMEM((ng, CAP, HEAD_DIM), jnp.bfloat16),
            pltpu.VMEM((128, 16), jnp.float32),
            pltpu.VMEM((ni, 8, HEAD_DIM), jnp.float32),
            pltpu.VMEM((no, 8, HEAD_DIM), jnp.float32),
            pltpu.VMEM((ng, 8, HEAD_DIM), jnp.float32),
            pltpu.SMEM(src_len.shape, jnp.int32),
            pltpu.SMEM(tgt_len.shape, jnp.int32),
            pltpu.SMEM((1, destination.shape[0]), jnp.int32),
            dma((3, CHUNKS)), dma((3,)), dma((ng,)), dma((ng,)), dma((ng,)), dma((ng,)), dma((2,)),
            dma((ni,)), dma((ni,)), dma((no,)), dma((no,)), dma((ng,)), dma((ng,)),
        ],
        compiler_params=pltpu.CompilerParams(
            collective_id=0, has_side_effects=True, vmem_limit_bytes=56 << 20
        ),
        cost_estimate=pl.CostEstimate(
            flops=4 * rows * depth * HEAD_DIM, bytes_accessed=12 << 20, transcendentals=1 << 19
        ),
    )(enc_out, w_key, w_value, queries, src_len, tgt_len, destination.reshape(1, -1))
    return context, variance.reshape(())


def solution(mesh):
    return jax.shard_map(
        functools.partial(per_device, mesh.shape["grp"], mesh.shape["mdl"]),
        mesh=mesh,
        in_specs=(P("grp", None), P(None, "mdl"), P(None, "mdl"), P("grp", "mdl"), P(), P(), P()),
        out_specs=(P("grp", "mdl"), P()),
        check_vma=False,
    )
```

```python
import functools
import math

import jax
import jax.numpy as jnp
from jax import lax
from jax.experimental import pallas as pl
from jax.experimental.pallas import tpu as pltpu
from jax.sharding import PartitionSpec as P

HEAD_DIM = 128
CAP = 96
SENTS = 19
CHUNKS = 8
BATCH = 4
MESH = pl.DeviceIdType.MESH
SCALE = math.log2(math.e) * HEAD_DIM**-0.5


def kernel(
    ng, nz,
    enc, wk, wv, q, src, tgt, dst,
    ctx, var,
    enc_v, w_v, q_v, c_v, seg_v, plane_v, line_v, src_s, tgt_s, dst_s,
    load_sem, small_sem, qs_sem, qr_sem, cs_sem, cr_sem, own_sem,
    ps_sem, pr_sem, ls_sem, lr_sem, near_sem,
):
    me = lax.axis_index("grp")
    mm = lax.axis_index("mdl")
    rows, depth = enc.shape
    kc = depth // CHUNKS
    z, core = mm // 2, lax.rem(mm, 2)

    def plane_peer(i):
        return {"grp": lax.rem(me + i % ng, ng), "mdl": z * 2 + lax.rem(core + i // ng, 2)}

    def line_peer(d):
        return {"mdl": lax.rem(z + d, nz) * 2 + core}

    def tell(sem, peer):
        pl.semaphore_signal(sem, inc=1, device_id=peer, device_id_type=MESH)

    barrier = pltpu.get_barrier_semaphore()
    for i in range(1, 2 * ng):
        tell(barrier, plane_peer(i))
    ends = sorted({1, nz - 1})
    for d in ends:
        tell(barrier, line_peer(d))

    steps = [2**k for k in range(max(nz.bit_length() - 2, 0))]

    def spread(k):
        for d in sorted({steps[k], nz - steps[k]}):
            tell(near_sem.at[k], line_peer(d))

    def heard(k):
        pl.semaphore_wait(near_sem.at[k], len({steps[k], nz - steps[k]}))
        if k + 1 < len(steps):
            spread(k + 1)

    small = [
        pltpu.make_async_copy(a, b, small_sem.at[i])
        for i, (a, b) in enumerate(((src, src_s), (tgt, tgt_s), (dst, dst_s)))
    ]
    for copy in small:
        copy.start()

    def loads(c):
        part = pl.ds(c * kc, kc)
        return (
            pltpu.make_async_copy(enc.at[:, part], enc_v.at[c], load_sem.at[0, c]),
            pltpu.make_async_copy(wk.at[part], w_v.at[part, pl.ds(0, HEAD_DIM)], load_sem.at[1, c]),
            pltpu.make_async_copy(
                wv.at[part], w_v.at[part, pl.ds(HEAD_DIM, HEAD_DIM)], load_sem.at[2, c]
            ),
        )

    own_rows = pl.ds(pl.multiple_of(me * CAP, 32), CAP)
    own_q = pltpu.make_async_copy(q.at[own_rows], q_v.at[0], own_sem.at[0])
    own_q.start()
    for c in range(CHUNKS):
        for copy in loads(c):
            copy.start()

    pl.semaphore_wait(barrier, 2 * ng - 1 + len(ends))

    def query_copy(d):
        peer = lax.rem(me + d, ng)
        return pltpu.make_async_remote_copy(
            src_ref=q.at[pl.ds(pl.multiple_of(peer * CAP, 32), CAP)],
            dst_ref=q_v.at[d],
            send_sem=qs_sem.at[d],
            recv_sem=qr_sem.at[d],
            device_id={"grp": peer},
            device_id_type=MESH,
        )

    for d in range(1, ng):
        query_copy(d).start()
    if steps:
        spread(0)

    for copy in small:
        copy.wait()
    slot = lax.broadcasted_iota(jnp.int32, seg_v.shape[::-1], 0)
    lane = lax.broadcasted_iota(jnp.int32, seg_v.shape[::-1], 1)
    group_of = lax.rem(me + ng - slot % ng, ng)
    key_row = lax.broadcasted_iota(jnp.int32, (1, rows), 1)
    seg_q = jnp.full(slot.shape, -1.0, jnp.float32)
    seg_k = jnp.zeros((1, rows), jnp.float32)
    filled = jnp.zeros(slot.shape, jnp.int32)
    start = jnp.int32(0)
    for i in range(SENTS):
        count = tgt_s[me * SENTS + i]
        going = group_of == dst_s[0, me * SENTS + i]
        after = jnp.where(going, filled + count, filled)
        seg_q = jnp.where((lane >= filled) & (lane < after), float(i), seg_q)
        filled = after
        seg_k = jnp.where(key_row >= start, float(i), seg_k)
        start = start + src_s[me, i]
    side = seg_v.shape[0]
    eye = (
        lax.broadcasted_iota(jnp.int32, (side, side), 0)
        == lax.broadcasted_iota(jnp.int32, (side, side), 1)
    ).astype(jnp.float32).astype(jnp.bfloat16)
    seg_v[...] = lax.dot_general(
        eye, seg_q.astype(jnp.bfloat16), (((1,), (1,)), ((), ())),
        preferred_element_type=jnp.float32,
    )
    live_rows = lax.fori_loop(
        0, tgt.shape[0], lambda i, t: t + tgt_s[i], jnp.int32(0), unroll=8
    )

    pending = list(range(len(steps)))
    if pending:
        heard(pending.pop(0))

    total = jnp.zeros((rows, 2 * HEAD_DIM), jnp.float32)
    for c in range(CHUNKS):
        for copy in loads(c):
            copy.wait()
        total = total + jnp.dot(
            enc_v[c], w_v[pl.ds(c * kc, kc), :], preferred_element_type=jnp.float32
        )
        if c % 4 == 3 and len(pending) > 1:
            heard(pending.pop(0))
    keys = total[:, :HEAD_DIM].astype(jnp.bfloat16)
    values = jnp.concatenate(
        [total[:, HEAD_DIM:].astype(jnp.bfloat16), jnp.ones((rows, HEAD_DIM), jnp.bfloat16)], axis=1
    )

    def context_copy(d):
        return pltpu.make_async_remote_copy(
            src_ref=c_v.at[d],
            dst_ref=ctx.at[own_rows],
            send_sem=cs_sem.at[d],
            recv_sem=cr_sem.at[d],
            device_id={"grp": lax.rem(me + ng - d, ng)},
            device_id_type=MESH,
        )

    squares = jnp.zeros((8, HEAD_DIM), jnp.float32)
    own_c = pltpu.make_async_copy(c_v.at[0], ctx.at[own_rows], own_sem.at[1])
    for first in range(0, ng, BATCH):
        slots = range(first, first + BATCH)
        for d in slots:
            if d == 0:
                own_q.wait()
            else:
                query_copy(d).wait_recv()
        block = q_v[first : first + BATCH].reshape(BATCH * CAP, HEAD_DIM)
        seg = jnp.concatenate([seg_v[0:CAP, d : d + 1] for d in slots], axis=0)
        scores = lax.dot_general(
            block, keys, (((1,), (1,)), ((), ())), preferred_element_type=jnp.float32
        )
        scores = jnp.where(seg == seg_k, scores, -1e30)
        top = jnp.max(scores, axis=1, keepdims=True)
        powers = jnp.exp2((scores - top) * SCALE).astype(jnp.bfloat16)
        both = jnp.dot(powers, values, preferred_element_type=jnp.float32)
        attended = both[:, :HEAD_DIM] / both[:, HEAD_DIM:]
        attended = jnp.where(seg >= 0.0, attended, 0.0)
        c_v[first : first + BATCH] = attended.astype(jnp.bfloat16).reshape(BATCH, CAP, HEAD_DIM)
        squares = squares + jnp.sum(
            (attended * attended).reshape(BATCH * CAP // 8, 8, HEAD_DIM), axis=0
        )

    def add_copy(held, row, send_sem, recv_sem, d, peer):
        return pltpu.make_async_remote_copy(
            src_ref=held.at[row],
            dst_ref=held.at[row],
            send_sem=send_sem.at[d],
            recv_sem=recv_sem.at[d],
            device_id=peer,
            device_id_type=MESH,
        )

    def plane_copy(i):
        return add_copy(plane_v, core * ng + me, ps_sem, pr_sem, i, plane_peer(i))

    def line_copy(d):
        return add_copy(line_v, z, ls_sem, lr_sem, d, line_peer(d))

    plane_v[core * ng + me] = jnp.sum(squares, axis=0, keepdims=True)
    for i in range(1, 2 * ng):
        plane_copy(i).start()
    own_c.start()
    for d in range(1, ng):
        context_copy(d).start()
    while pending:
        heard(pending.pop(0))
    for i in range(1, 2 * ng):
        plane_copy(i).wait_recv()
    line_v[z] = jnp.sum(plane_v[...], axis=0)
    order = sorted(range(1, nz), key=lambda d: -min(d, nz - d))
    for d in order:
        line_copy(d).start()

    for i in range(1, 2 * ng):
        plane_copy(i).wait_send()
    own_c.wait()
    for d in range(1, ng):
        query_copy(d).wait_send()
        context_copy(d).wait()
    for d in range(1, nz):
        line_copy(d).wait()
    width = jnp.float32(HEAD_DIM * 2 * nz)
    var[...] = jnp.full(
        var.shape, jnp.sum(line_v[...]) / (width * live_rows.astype(jnp.float32)), jnp.float32
    )


def per_device(ng, nm, enc_out, w_key, w_value, queries, src_len, tgt_len, destination):
    nz = nm // 2
    rows, depth = enc_out.shape
    hbm = pl.BlockSpec(memory_space=pltpu.HBM)
    dma = pltpu.SemaphoreType.DMA
    context, variance = pl.pallas_call(
        functools.partial(kernel, ng, nz),
        name="attend",
        out_shape=(
            jax.ShapeDtypeStruct(queries.shape, jnp.bfloat16),
            jax.ShapeDtypeStruct((1, 1), jnp.float32),
        ),
        in_specs=[hbm] * 7,
        out_specs=(pl.BlockSpec(memory_space=pl.ANY), pl.BlockSpec(memory_space=pltpu.VMEM)),
        scratch_shapes=[
            pltpu.VMEM((CHUNKS, rows, depth // CHUNKS), jnp.bfloat16),
            pltpu.VMEM((depth, 2 * HEAD_DIM), jnp.bfloat16),
            pltpu.VMEM((ng, CAP, HEAD_DIM), jnp.bfloat16),
            pltpu.VMEM((ng, CAP, HEAD_DIM), jnp.bfloat16),
            pltpu.VMEM((128, 16), jnp.float32),
            pltpu.VMEM((2 * ng, 1, HEAD_DIM), jnp.float32),
            pltpu.VMEM((nz, 1, HEAD_DIM), jnp.float32),
            pltpu.SMEM(src_len.shape, jnp.int32),
            pltpu.SMEM(tgt_len.shape, jnp.int32),
            pltpu.SMEM((1, destination.shape[0]), jnp.int32),
            dma((3, CHUNKS)), dma((3,)), dma((ng,)), dma((ng,)), dma((ng,)), dma((ng,)), dma((2,)),
            dma((2 * ng,)), dma((2 * ng,)), dma((nz,)), dma((nz,)),
            pltpu.SemaphoreType.REGULAR((max(nz.bit_length() - 2, 1),)),
        ],
        compiler_params=pltpu.CompilerParams(
            collective_id=0, has_side_effects=True, vmem_limit_bytes=56 << 20
        ),
        cost_estimate=pl.CostEstimate(
            flops=4 * rows * depth * HEAD_DIM, bytes_accessed=12 << 20, transcendentals=1 << 19
        ),
    )(enc_out, w_key, w_value, queries, src_len, tgt_len, destination.reshape(1, -1))
    return context, variance.reshape(())


def solution(mesh):
    return jax.shard_map(
        functools.partial(per_device, mesh.shape["grp"], mesh.shape["mdl"]),
        mesh=mesh,
        in_specs=(P("grp", None), P(None, "mdl"), P(None, "mdl"), P("grp", "mdl"), P(), P(), P()),
        out_specs=(P("grp", "mdl"), P()),
        check_vma=False,
    )
```

```python
import functools
import math

import jax
import jax.numpy as jnp
from jax import lax
from jax.experimental import pallas as pl
from jax.experimental.pallas import tpu as pltpu
from jax.sharding import PartitionSpec as P

HEAD_DIM = 128
CAP = 96
SENTS = 19
CHUNKS = 8
EARLY = 2
NEAR = 4
MESH = pl.DeviceIdType.MESH
SCALE = math.log2(math.e) * HEAD_DIM**-0.5


def kernel(
    ng, nz,
    enc, wk, wv, q, src, tgt, dst,
    ctx, var,
    enc_v, w_v, q_v, c_v, pick_v, plane_v, line_v, src_s, tgt_s, dst_s,
    load_sem, small_sem, qs_sem, qr_sem, cs_sem, cr_sem, own_sem,
    ps_sem, pr_sem, ls_sem, lr_sem, near_sem,
):
    me = lax.axis_index("grp")
    mm = lax.axis_index("mdl")
    rows, depth = enc.shape
    kc = depth // CHUNKS
    z, core = mm // 2, lax.rem(mm, 2)

    side = math.isqrt(ng)
    y, x = me // side, lax.rem(me, side)

    def ahead(d):
        return lax.rem(y + d // side, side) * side + lax.rem(x + d % side, side)

    def behind(d):
        dy, dx = lax.div(d, side), lax.rem(d, side)
        return lax.rem(y + side - dy, side) * side + lax.rem(x + side - dx, side)

    def hops(d):
        dy, dx = d % ng // side, d % side
        return min(dy, side - dy) + min(dx, side - dx)

    far_groups = sorted(range(1, ng), key=hops, reverse=True)
    far_plane = sorted(range(1, 2 * ng), key=hops, reverse=True)

    def plane_peer(i):
        return {"grp": ahead(i % ng), "mdl": z * 2 + lax.rem(core + i // ng, 2)}

    def line_peer(d):
        return {"mdl": lax.rem(z + d, nz) * 2 + core}

    def tell(sem, peer):
        pl.semaphore_signal(sem, inc=1, device_id=peer, device_id_type=MESH)

    near = min(NEAR, nz // 2)

    def at_distance(k):
        return sorted({k, nz - k})

    close = [d for k in range(near, 0, -1) for d in at_distance(k)]
    barrier = pltpu.get_barrier_semaphore()
    for i in far_plane[: len(far_plane) // 2]:
        tell(barrier, plane_peer(i))
    for d in close:
        tell(barrier, line_peer(d))
    for i in far_plane[len(far_plane) // 2 :]:
        tell(barrier, plane_peer(i))

    steps = [near << k for k in range(nz.bit_length()) if (near << k) < nz // 2]

    def spread(k):
        for d in at_distance(steps[k]):
            tell(near_sem.at[k], line_peer(d))

    def heard(k):
        if k < len(steps):
            pl.semaphore_wait(near_sem.at[k], len(at_distance(steps[k])))
            if k + 1 < len(steps):
                spread(k + 1)

    small = [
        pltpu.make_async_copy(a, b, small_sem.at[i])
        for i, (a, b) in enumerate(((src, src_s), (tgt, tgt_s), (dst, dst_s)))
    ]
    for copy in small:
        copy.start()

    def loads(c):
        part = pl.ds(c * kc, kc)
        return (
            pltpu.make_async_copy(enc.at[:, part], enc_v.at[c], load_sem.at[0, c]),
            pltpu.make_async_copy(wk.at[part], w_v.at[part, pl.ds(0, HEAD_DIM)], load_sem.at[1, c]),
            pltpu.make_async_copy(
                wv.at[part], w_v.at[part, pl.ds(HEAD_DIM, HEAD_DIM)], load_sem.at[2, c]
            ),
        )

    own_rows = pl.ds(pl.multiple_of(me * CAP, 32), CAP)
    own_q = pltpu.make_async_copy(q.at[own_rows], q_v.at[0], own_sem.at[0])
    own_q.start()
    for c in range(CHUNKS):
        for copy in loads(c):
            copy.start()

    def query_copy(d):
        peer = ahead(d)
        return pltpu.make_async_remote_copy(
            src_ref=q.at[pl.ds(pl.multiple_of(peer * CAP, 32), CAP)],
            dst_ref=q_v.at[d],
            send_sem=qs_sem.at[d],
            recv_sem=qr_sem.at[d],
            device_id={"grp": peer},
            device_id_type=MESH,
        )

    for copy in small:
        copy.wait()
    slot = lax.broadcasted_iota(jnp.int32, (ng, 128), 0)
    lane = lax.broadcasted_iota(jnp.int32, (ng, 128), 1)
    group_of = behind(slot)
    key_row = lax.broadcasted_iota(jnp.int32, (1, rows), 1)
    target_row = lax.broadcasted_iota(jnp.int32, (rows, 1), 0)
    place = jnp.full(slot.shape, -1, jnp.int32)
    seg_k = jnp.zeros((1, rows), jnp.int32)
    seg_q = jnp.zeros((rows, 1), jnp.int32)
    filled = jnp.zeros(slot.shape, jnp.int32)
    start = jnp.int32(0)
    first = jnp.int32(0)
    for i in range(SENTS):
        count = tgt_s[me * SENTS + i]
        going = group_of == dst_s[0, me * SENTS + i]
        after = jnp.where(going, filled + count, filled)
        place = jnp.where((lane >= filled) & (lane < after), lane - filled + first, place)
        filled = after
        seg_k = jnp.where(key_row >= start, i, seg_k)
        seg_q = jnp.where(target_row >= first, i, seg_q)
        start = start + src_s[me, i]
        first = first + count
    place = place.astype(jnp.float32)
    across = place.T
    order_row = lax.broadcasted_iota(jnp.int32, (rows, CAP), 0).astype(jnp.float32)
    for d in range(ng):
        pick_v[d] = jnp.where(order_row == place[d : d + 1, :CAP], 1.0, 0.0).astype(jnp.bfloat16)
    live_rows = lax.fori_loop(
        0, tgt.shape[0], lambda i, t: t + tgt_s[i], jnp.int32(0), unroll=8
    )

    total = jnp.zeros((rows, 2 * HEAD_DIM), jnp.float32)
    for c in range(CHUNKS):
        if c == EARLY:
            pl.semaphore_wait(barrier, 2 * ng - 1 + len(close))
            for d in far_groups:
                query_copy(d).start()
            if steps:
                spread(0)
        for copy in loads(c):
            copy.wait()
        total = total + jnp.dot(
            enc_v[c], w_v[pl.ds(c * kc, kc), :], preferred_element_type=jnp.float32
        )
    heard(0)
    keys = total[:, :HEAD_DIM].astype(jnp.bfloat16)
    values = jnp.concatenate(
        [total[:, HEAD_DIM:].astype(jnp.bfloat16), jnp.ones((rows, HEAD_DIM), jnp.bfloat16)], axis=1
    )

    def context_copy(d):
        return pltpu.make_async_remote_copy(
            src_ref=c_v.at[d],
            dst_ref=ctx.at[own_rows],
            send_sem=cs_sem.at[d],
            recv_sem=cr_sem.at[d],
            device_id={"grp": behind(d)},
            device_id_type=MESH,
        )

    gathered = jnp.zeros((rows, HEAD_DIM), jnp.float32)
    for d in [0] + far_groups[::-1]:
        if d == 0:
            own_q.wait()
        else:
            query_copy(d).wait_recv()
        gathered = gathered + jnp.dot(pick_v[d], q_v[d], preferred_element_type=jnp.float32)
    scores = lax.dot_general(
        gathered.astype(jnp.bfloat16), keys, (((1,), (1,)), ((), ())),
        preferred_element_type=jnp.float32,
    )
    scores = jnp.where(seg_q == seg_k, scores, -1e30)
    top = jnp.max(scores, axis=1, keepdims=True)
    powers = jnp.exp2((scores - top) * SCALE).astype(jnp.bfloat16)
    both = jnp.dot(powers, values, preferred_element_type=jnp.float32)
    attended = both[:, :HEAD_DIM] / both[:, HEAD_DIM:]
    attended = jnp.where(target_row < first, attended, 0.0)
    squares = attended * attended

    def add_copy(held, row, send_sem, recv_sem, d, peer):
        return pltpu.make_async_remote_copy(
            src_ref=held.at[row],
            dst_ref=held.at[row],
            send_sem=send_sem.at[d],
            recv_sem=recv_sem.at[d],
            device_id=peer,
            device_id_type=MESH,
        )

    def plane_copy(i):
        return add_copy(plane_v, core * ng + me, ps_sem, pr_sem, i, plane_peer(i))

    def line_copy(d):
        return add_copy(line_v, z, ls_sem, lr_sem, d, line_peer(d))

    plane_v[core * ng + me] = jnp.sum(squares, axis=0, keepdims=True)
    for i in far_plane:
        plane_copy(i).start()
    own_c = pltpu.make_async_copy(c_v.at[0], ctx.at[own_rows], own_sem.at[1])
    attended = attended.astype(jnp.bfloat16)
    order_lane = lax.broadcasted_iota(jnp.int32, (CAP, rows), 1).astype(jnp.float32)
    for d in far_groups + [0]:
        spread_out = jnp.where(order_lane == across[:CAP, d : d + 1], 1.0, 0.0)
        c_v[d] = jnp.dot(
            spread_out.astype(jnp.bfloat16), attended, preferred_element_type=jnp.float32
        ).astype(jnp.bfloat16)
        if d == 0:
            own_c.start()
        else:
            context_copy(d).start()
    for i in range(1, 2 * ng):
        plane_copy(i).wait_recv()
    for k in range(1, len(steps)):
        heard(k)
    line_v[z] = jnp.sum(plane_v[...], axis=0)
    order = sorted(range(1, nz), key=lambda d: -min(d, nz - d))
    for d in order:
        line_copy(d).start()

    for i in range(1, 2 * ng):
        plane_copy(i).wait_send()
    own_c.wait()
    for d in range(1, ng):
        query_copy(d).wait_send()
        context_copy(d).wait()
    for d in range(1, nz):
        line_copy(d).wait()
    width = jnp.float32(HEAD_DIM * 2 * nz)
    var[...] = jnp.full(
        var.shape, jnp.sum(line_v[...]) / (width * live_rows.astype(jnp.float32)), jnp.float32
    )


def per_device(ng, nm, enc_out, w_key, w_value, queries, src_len, tgt_len, destination):
    nz = nm // 2
    rows, depth = enc_out.shape
    hbm = pl.BlockSpec(memory_space=pltpu.HBM)
    dma = pltpu.SemaphoreType.DMA
    context, variance = pl.pallas_call(
        functools.partial(kernel, ng, nz),
        name="attend",
        out_shape=(
            pltpu.VMEM(queries.shape, jnp.bfloat16),
            pltpu.VMEM((1, 1), jnp.float32),
        ),
        in_specs=[hbm] * 7,
        out_specs=(pl.BlockSpec(memory_space=pl.ANY), pl.BlockSpec(memory_space=pltpu.VMEM)),
        scratch_shapes=[
            pltpu.VMEM((CHUNKS, rows, depth // CHUNKS), jnp.bfloat16),
            pltpu.VMEM((depth, 2 * HEAD_DIM), jnp.bfloat16),
            pltpu.VMEM((ng, CAP, HEAD_DIM), jnp.bfloat16),
            pltpu.VMEM((ng, CAP, HEAD_DIM), jnp.bfloat16),
            pltpu.VMEM((ng, rows, CAP), jnp.bfloat16),
            pltpu.VMEM((2 * ng, 1, HEAD_DIM), jnp.float32),
            pltpu.VMEM((nz, 1, HEAD_DIM), jnp.float32),
            pltpu.SMEM(src_len.shape, jnp.int32),
            pltpu.SMEM(tgt_len.shape, jnp.int32),
            pltpu.SMEM((1, destination.shape[0]), jnp.int32),
            dma((3, CHUNKS)), dma((3,)), dma((ng,)), dma((ng,)), dma((ng,)), dma((ng,)), dma((2,)),
            dma((2 * ng,)), dma((2 * ng,)), dma((nz,)), dma((nz,)),
            pltpu.SemaphoreType.REGULAR((nz.bit_length(),)),
        ],
        compiler_params=pltpu.CompilerParams(
            collective_id=0, has_side_effects=True, vmem_limit_bytes=56 << 20
        ),
        cost_estimate=pl.CostEstimate(
            flops=4 * rows * depth * HEAD_DIM, bytes_accessed=12 << 20, transcendentals=1 << 19
        ),
    )(enc_out, w_key, w_value, queries, src_len, tgt_len, destination.reshape(1, -1))
    return context, variance.reshape(())


def solution(mesh):
    return jax.shard_map(
        functools.partial(per_device, mesh.shape["grp"], mesh.shape["mdl"]),
        mesh=mesh,
        in_specs=(P("grp", None), P(None, "mdl"), P(None, "mdl"), P("grp", "mdl"), P(), P(), P()),
        out_specs=(P("grp", "mdl"), P()),
        check_vma=False,
    )
```

```python
import functools
import math

import jax
import jax.numpy as jnp
from jax import lax
from jax.experimental import pallas as pl
from jax.experimental.pallas import tpu as pltpu
from jax.sharding import PartitionSpec as P

HEAD_DIM = 128
CAP = 96
SENTS = 19
CHUNKS = 8
NEAR = 4
MESH = pl.DeviceIdType.MESH
SCALE = math.log2(math.e) * HEAD_DIM**-0.5


def kernel(
    ng, nz,
    enc, wk, wv, q, src, tgt, dst,
    ctx, var,
    enc_v, w_v, q_v, c_v, pick_v, plane_v, line_v, src_s, tgt_s, dst_s,
    load_sem, small_sem, qs_sem, qr_sem, cs_sem, cr_sem, own_sem,
    ps_sem, pr_sem, ls_sem, lr_sem, near_sem, core_sem,
):
    me = lax.axis_index("grp")
    mm = lax.axis_index("mdl")
    rows, depth = enc.shape
    kc = depth // CHUNKS
    z, core = mm // 2, lax.rem(mm, 2)

    side = math.isqrt(ng)
    y, x = me // side, lax.rem(me, side)
    ys = [lax.rem(y + k, side) * side for k in range(side)]
    xs = [lax.rem(x + k, side) for k in range(side)]

    def ahead(d):
        return ys[d // side] + xs[d % side]

    def behind(d):
        dy, dx = lax.div(d, side), lax.rem(d, side)
        return lax.rem(y + side - dy, side) * side + lax.rem(x + side - dx, side)

    def hops(d):
        dy, dx = d % ng // side, d % side
        return min(dy, side - dy) + min(dx, side - dx)

    far_groups = sorted(range(1, ng), key=hops, reverse=True)
    far_plane = sorted(range(1, 2 * ng), key=hops, reverse=True)

    def plane_peer(i):
        return {"grp": ahead(i % ng), "mdl": mm if i < ng else z * 2 + 1 - core}

    def line_peer(d):
        return {"mdl": lax.rem(z + d, nz) * 2 + core}

    def tell(sem, peer):
        pl.semaphore_signal(sem, inc=1, device_id=peer, device_id_type=MESH)

    near = min(NEAR, nz // 2)

    def at_distance(k):
        return sorted({k, nz - k})

    close = [d for k in range(near, 0, -1) for d in at_distance(k)]
    barrier = pltpu.get_barrier_semaphore()
    for i in far_groups + [ng]:
        tell(barrier, plane_peer(i))
    for d in close:
        tell(barrier, line_peer(d))

    steps = [near << k for k in range(nz.bit_length()) if (near << k) < nz // 2]

    def spread(k):
        for d in at_distance(steps[k]):
            tell(near_sem.at[k], line_peer(d))

    def heard(k):
        if k < len(steps):
            pl.semaphore_wait(near_sem.at[k], len(at_distance(steps[k])))
            if k + 1 < len(steps):
                spread(k + 1)

    small = [
        pltpu.make_async_copy(a, b, small_sem.at[i])
        for i, (a, b) in enumerate(((src, src_s), (tgt, tgt_s), (dst, dst_s)))
    ]
    for copy in small:
        copy.start()

    def loads(c):
        part = pl.ds(c * kc, kc)
        return (
            pltpu.make_async_copy(enc.at[:, part], enc_v.at[c], load_sem.at[0, c]),
            pltpu.make_async_copy(wk.at[part], w_v.at[part, pl.ds(0, HEAD_DIM)], load_sem.at[1, c]),
            pltpu.make_async_copy(
                wv.at[part], w_v.at[part, pl.ds(HEAD_DIM, HEAD_DIM)], load_sem.at[2, c]
            ),
        )

    own_rows = pl.ds(pl.multiple_of(me * CAP, 32), CAP)
    own_q = pltpu.make_async_copy(q.at[own_rows], q_v.at[0], own_sem.at[0])
    own_q.start()
    for c in range(CHUNKS):
        for copy in loads(c):
            copy.start()

    def query_copy(d):
        peer = ahead(d)
        return pltpu.make_async_remote_copy(
            src_ref=q.at[pl.ds(pl.multiple_of(peer * CAP, 32), CAP)],
            dst_ref=q_v.at[d],
            send_sem=qs_sem.at[d],
            recv_sem=qr_sem.at[d],
            device_id={"grp": peer},
            device_id_type=MESH,
        )

    for copy in small:
        copy.wait()
    slot = lax.broadcasted_iota(jnp.int32, (ng, 128), 0)
    lane = lax.broadcasted_iota(jnp.int32, (ng, 128), 1)
    group_of = behind(slot)
    key_row = lax.broadcasted_iota(jnp.int32, (1, rows), 1)
    target_row = lax.broadcasted_iota(jnp.int32, (rows, 1), 0)
    place = jnp.full(slot.shape, -1, jnp.int32)
    seg_k = jnp.zeros((1, rows), jnp.int32)
    begins = []
    filled = jnp.zeros(slot.shape, jnp.int32)
    start = jnp.int32(0)
    first = jnp.int32(0)
    for i in range(SENTS):
        count = tgt_s[me * SENTS + i]
        going = group_of == dst_s[0, me * SENTS + i]
        after = jnp.where(going, filled + count, filled)
        place = jnp.where((lane >= filled) & (lane < after), lane - filled + first, place)
        filled = after
        seg_k = jnp.where(key_row >= start, i, seg_k)
        begins.append((first, i))
        start = start + src_s[me, i]
        first = first + count

    pl.semaphore_wait(barrier, ng + len(close))
    for d in far_groups[::-1]:
        query_copy(d).start()
    tell(core_sem, plane_peer(ng))
    if steps:
        spread(0)

    seg_q = jnp.zeros((rows, 1), jnp.int32)
    for begin, i in begins:
        seg_q = jnp.where(target_row >= begin, i, seg_q)
    place = place.astype(jnp.float32)
    across = place.T
    order_row = lax.broadcasted_iota(jnp.int32, (rows, CAP), 0).astype(jnp.float32)
    for d in range(ng):
        pick_v[d] = jnp.where(order_row == place[d : d + 1, :CAP], 1.0, 0.0).astype(jnp.bfloat16)

    total = jnp.zeros((rows, 2 * HEAD_DIM), jnp.float32)
    for c in range(CHUNKS):
        for copy in loads(c):
            copy.wait()
        total = total + jnp.dot(
            enc_v[c], w_v[pl.ds(c * kc, kc), :], preferred_element_type=jnp.float32
        )
    pl.semaphore_wait(core_sem, 1)
    heard(0)
    keys = total[:, :HEAD_DIM].astype(jnp.bfloat16)
    values = jnp.concatenate(
        [total[:, HEAD_DIM:].astype(jnp.bfloat16), jnp.ones((rows, HEAD_DIM), jnp.bfloat16)], axis=1
    )

    def context_copy(d):
        return pltpu.make_async_remote_copy(
            src_ref=c_v.at[d],
            dst_ref=ctx.at[own_rows],
            send_sem=cs_sem.at[d],
            recv_sem=cr_sem.at[d],
            device_id={"grp": behind(d)},
            device_id_type=MESH,
        )

    gathered = jnp.zeros((rows, HEAD_DIM), jnp.float32)
    for d in [0] + far_groups[::-1]:
        if d == 0:
            own_q.wait()
        else:
            query_copy(d).wait_recv()
        gathered = gathered + jnp.dot(pick_v[d], q_v[d], preferred_element_type=jnp.float32)
    scores = lax.dot_general(
        gathered.astype(jnp.bfloat16), keys, (((1,), (1,)), ((), ())),
        preferred_element_type=jnp.float32,
    )
    scores = jnp.where(seg_q == seg_k, scores, -1e30)
    top = jnp.max(scores, axis=1, keepdims=True)
    powers = jnp.exp2((scores - top) * SCALE).astype(jnp.bfloat16)
    both = jnp.dot(powers, values, preferred_element_type=jnp.float32)
    attended = both[:, :HEAD_DIM] / both[:, HEAD_DIM:]
    attended = jnp.where(target_row < first, attended, 0.0)
    squares = attended * attended

    def add_copy(held, row, send_sem, recv_sem, d, peer):
        return pltpu.make_async_remote_copy(
            src_ref=held.at[row],
            dst_ref=held.at[row],
            send_sem=send_sem.at[d],
            recv_sem=recv_sem.at[d],
            device_id=peer,
            device_id_type=MESH,
        )

    def plane_copy(i):
        return add_copy(plane_v, core * ng + me, ps_sem, pr_sem, i, plane_peer(i))

    def line_copy(d):
        return add_copy(line_v, z, ls_sem, lr_sem, d, line_peer(d))

    plane_v[core * ng + me] = jnp.sum(squares, axis=0, keepdims=True)
    for i in far_plane:
        plane_copy(i).start()
    own_c = pltpu.make_async_copy(c_v.at[0], ctx.at[own_rows], own_sem.at[1])
    attended = attended.astype(jnp.bfloat16)
    order_lane = lax.broadcasted_iota(jnp.int32, (CAP, rows), 1).astype(jnp.float32)
    for d in far_groups + [0]:
        spread_out = jnp.where(order_lane == across[:CAP, d : d + 1], 1.0, 0.0)
        c_v[d] = jnp.dot(
            spread_out.astype(jnp.bfloat16), attended, preferred_element_type=jnp.float32
        ).astype(jnp.bfloat16)
        if d == 0:
            own_c.start()
        else:
            context_copy(d).start()
    for i in range(1, 2 * ng):
        plane_copy(i).wait_recv()
    for k in range(1, len(steps)):
        heard(k)
    line_v[z] = jnp.sum(plane_v[...], axis=0)
    order = sorted(range(1, nz), key=lambda d: -min(d, nz - d))
    for d in order:
        line_copy(d).start()
    live_rows = lax.fori_loop(
        0, tgt.shape[0], lambda i, t: t + tgt_s[i], jnp.int32(0), unroll=8
    )

    for i in range(1, 2 * ng):
        plane_copy(i).wait_send()
    own_c.wait()
    for d in range(1, ng):
        query_copy(d).wait_send()
        context_copy(d).wait()
    for d in range(1, nz):
        line_copy(d).wait_send()
    for d in order[::-1]:
        line_copy(d).wait_recv()
    width = jnp.float32(HEAD_DIM * 2 * nz)
    var[...] = jnp.full(
        var.shape, jnp.sum(line_v[...]) / (width * live_rows.astype(jnp.float32)), jnp.float32
    )


def per_device(ng, nm, enc_out, w_key, w_value, queries, src_len, tgt_len, destination):
    nz = nm // 2
    rows, depth = enc_out.shape
    hbm = pl.BlockSpec(memory_space=pltpu.HBM)
    dma = pltpu.SemaphoreType.DMA
    context, variance = pl.pallas_call(
        functools.partial(kernel, ng, nz),
        name="attend",
        out_shape=(
            pltpu.VMEM(queries.shape, jnp.bfloat16),
            pltpu.VMEM((1, 1), jnp.float32),
        ),
        in_specs=[hbm] * 7,
        out_specs=(pl.BlockSpec(memory_space=pl.ANY), pl.BlockSpec(memory_space=pltpu.VMEM)),
        scratch_shapes=[
            pltpu.VMEM((CHUNKS, rows, depth // CHUNKS), jnp.bfloat16),
            pltpu.VMEM((depth, 2 * HEAD_DIM), jnp.bfloat16),
            pltpu.VMEM((ng, CAP, HEAD_DIM), jnp.bfloat16),
            pltpu.VMEM((ng, CAP, HEAD_DIM), jnp.bfloat16),
            pltpu.VMEM((ng, rows, CAP), jnp.bfloat16),
            pltpu.VMEM((2 * ng, 1, HEAD_DIM), jnp.float32),
            pltpu.VMEM((nz, 1, HEAD_DIM), jnp.float32),
            pltpu.SMEM(src_len.shape, jnp.int32),
            pltpu.SMEM(tgt_len.shape, jnp.int32),
            pltpu.SMEM((1, destination.shape[0]), jnp.int32),
            dma((3, CHUNKS)), dma((3,)), dma((ng,)), dma((ng,)), dma((ng,)), dma((ng,)), dma((2,)),
            dma((2 * ng,)), dma((2 * ng,)), dma((nz,)), dma((nz,)),
            pltpu.SemaphoreType.REGULAR((nz.bit_length(),)),
            pltpu.SemaphoreType.REGULAR,
        ],
        compiler_params=pltpu.CompilerParams(
            collective_id=0, has_side_effects=True, vmem_limit_bytes=56 << 20
        ),
        cost_estimate=pl.CostEstimate(
            flops=4 * rows * depth * HEAD_DIM, bytes_accessed=12 << 20, transcendentals=1 << 19
        ),
    )(enc_out, w_key, w_value, queries, src_len, tgt_len, destination.reshape(1, -1))
    return context, variance.reshape(())


def solution(mesh):
    return jax.shard_map(
        functools.partial(per_device, mesh.shape["grp"], mesh.shape["mdl"]),
        mesh=mesh,
        in_specs=(P("grp", None), P(None, "mdl"), P(None, "mdl"), P("grp", "mdl"), P(), P(), P()),
        out_specs=(P("grp", "mdl"), P()),
        check_vma=False,
    )
```
